32 devices in a mesh: dp: 32 (over z, y, x, core), width: 1.
Axes of the slice: x: 2, y: 2, z: 4, core: 2. Of those that a mesh axis runs over, the one named last changes fastest.
Arguments:
- activations: bfloat16 [16384, 5120], P('dp', 'width'), may hold values from -6 to 6
- gradients: bfloat16 [16384, 5120], P('dp', 'width'), may hold values from -1.5 to 1.5, as said below
- in_basis: float32 [2560, 5120], P('dp', 'width'), may hold values from -0.078125 to 0.078125
- out_basis: float32 [2560, 5120], P('dp', 'width'), may hold values from -0.078125 to 0.078125
Outputs:
- preconditioned: bfloat16 [32, 2560, 2560], P('dp', None, 'width')
- eigenvalues: float32 [2560, 2560], P('dp', 'width')
The draws below stay inside these ranges and needn't reach their ends.
Inputs may be any that keep to these rules, and one draw needn't show every extreme that they name: Output gradients of the layer.
All inputs are finite; a program needn't handle non-finite values.
Results may differ from the reference program's by a relative error of at most 0.0074.
Values may be sent and summed in bfloat16 or wider, within the bound.
A program may use at most 192 MiB of HBM per device.

```python
import jax
import jax.numpy as jnp
from jax import lax

D = 5120
KI = 2560
KO = 2560
SEQ_LEN = 512
SEQS = 32
TOKENS = 16384


def draw_gradients(key, part):
    key_scale, key_base = jax.random.split(jax.random.fold_in(key, 11), 2)
    seq_scale = jnp.exp(jax.random.uniform(key_scale, (SEQS, 1, 1), jnp.float32, jnp.log(0.3), jnp.log(3.0)))
    base_vals = jax.random.normal(key_base, (SEQS, SEQ_LEN, D), jnp.float32)
    values = base_vals * seq_scale / jnp.sqrt(jnp.float32(SEQ_LEN))
    values = jnp.clip(values, -1.5, 1.5)
    return values.reshape(SEQS * SEQ_LEN, D).astype(jnp.bfloat16)


def shard_levels(rng, extent, cuts, smallest, high):
    gain, own = 1.0, jax.random.fold_in(rng, 6)
    for axis_at, blocks in cuts:
        steps = jnp.exp(jax.random.uniform(jax.random.fold_in(own, axis_at), (blocks,), jnp.float32, smallest / len(cuts), high / len(cuts)))
        gain = gain * jnp.repeat(steps, extent[axis_at] // blocks).reshape([-1 if axis == axis_at else 1 for axis in range(len(extent))])
    return gain


def gaussian(rng, extent, spread, reach, cuts=(), dtype=jnp.bfloat16):
    drawn = jax.random.normal(rng, extent, jnp.float32) * spread
    if len(cuts) > 0:
        drawn = shard_levels(rng, extent, cuts, -0.22, 0.18) * drawn
    return jnp.clip(drawn, min=-reach, max=reach).astype(dtype)


def setup_inputs(seed: int = 0) -> dict:
    keys = jax.random.split(jax.random.key(seed), 5)
    return {
        "activations": gaussian(keys[0], (TOKENS, D), 1.0, 6.0, ((0, 32),)),
        "gradients": draw_gradients(jax.random.fold_in(keys[4], 71), 0),
        "in_basis": gaussian(keys[2], (KI, D), D ** -0.5, 0.078125, ((0, 32),), jnp.float32),
        "out_basis": gaussian(keys[3], (KO, D), D ** -0.5, 0.078125, ((0, 32),), jnp.float32),
    }


damping = 0.1


def reference(activations, gradients, in_basis, out_basis):
    in_narrow = in_basis.astype(jnp.bfloat16)
    out_narrow = out_basis.astype(jnp.bfloat16)
    in_rotated = jnp.dot(activations, in_narrow.T, preferred_element_type=jnp.float32).astype(jnp.bfloat16)
    out_rotated = jnp.dot(gradients, out_narrow.T, preferred_element_type=jnp.float32).astype(jnp.bfloat16)
    in_seq = in_rotated.reshape(SEQS, SEQ_LEN, KI)
    out_seq = out_rotated.reshape(SEQS, SEQ_LEN, KO)

    def accumulate(summed, batch_pair):
        product = jnp.dot(batch_pair[1].T, batch_pair[0], preferred_element_type=jnp.float32)
        return summed + product * product, None

    summed, unused = lax.scan(accumulate, jnp.zeros((KO, KI), jnp.float32), (in_seq, out_seq))
    eigenvalues = summed / SEQS
    inverse = 1.0 / (eigenvalues + damping)

    def scaled(batch_pair):
        product = jnp.dot(batch_pair[1].T, batch_pair[0], preferred_element_type=jnp.float32)
        return (product * inverse).astype(jnp.bfloat16)

    preconditioned = lax.map(scaled, (in_seq, out_seq))
    return preconditioned, eigenvalues
```

```python
import jax
import jax.numpy as jnp
from jax import lax
from jax.sharding import PartitionSpec as P

SEQ_LEN = 512


damping = 0.1


def rotate(source, tile_rows):
    return lax.dot_general(
        source, tile_rows, (((1,), (1,)), ((), ())), preferred_element_type=jnp.float32
    )


def rotate_both(activations, gradients, in_basis, out_basis):
    partial_in = rotate(
        activations, lax.all_gather(in_basis.astype(jnp.bfloat16), "dp", axis=0, tiled=True)
    )
    in_rotated = lax.psum_scatter(partial_in, "width", scatter_dimension=1, tiled=True).astype(
        jnp.bfloat16
    )
    partial_out = rotate(
        gradients, lax.all_gather(out_basis.astype(jnp.bfloat16), "dp", axis=0, tiled=True)
    )
    shared = lax.psum_scatter(partial_out, "width", scatter_dimension=1, tiled=True).astype(
        jnp.bfloat16
    )
    return in_rotated, lax.all_gather(shared, "width", axis=1, tiled=True)


def bit_set(bit):
    return (lax.axis_index("dp") // (1 << bit)) % 2 == 1


def swap(block, bit):
    size = lax.axis_size("dp")
    return lax.ppermute(block, "dp", [(d, d ^ (1 << bit)) for d in range(size)])


def hop_orders(bits):
    if bits == 5:
        return [(3, 1, 4, 2), (4, 2, 3, 1)]
    hops = tuple(range(1, bits))
    return [hops[i:] + hops[:i] for i in range(len(hops))] or [()]


def scatter_pieces(pieces, orders):
    held, left = list(pieces), [sorted(order, reverse=True) for order in orders]
    for stage in range(len(orders[0])):
        for i, order in enumerate(orders):
            bit = order[stage]
            axis = left[i].index(bit)
            left[i].pop(axis)
            up = bit_set(bit)
            low = lax.index_in_dim(held[i], 0, axis, keepdims=False)
            high = lax.index_in_dim(held[i], 1, axis, keepdims=False)
            got = swap(jnp.where(up, low, high).astype(jnp.bfloat16), bit)
            held[i] = jnp.where(up, high, low).astype(jnp.float32) + got.astype(jnp.float32)
            if stage < len(orders[0]) - 1:
                held[i] = held[i].astype(jnp.bfloat16)
    return held


def outer(in_rotated, out_rotated, seq_here):
    in_seq = in_rotated.reshape(seq_here, SEQ_LEN, in_rotated.shape[1])
    out_seq = out_rotated.reshape(seq_here, SEQ_LEN, out_rotated.shape[1])
    return jnp.einsum("nlo,nlk->nok", out_seq, in_seq, preferred_element_type=jnp.float32)


def row_chunks(rows):
    last = rows * 2 // 5 // 16 * 16
    return [(0, rows - last), (rows - last, rows)] if last > 0 else [(0, rows)]


def on_device(activations, gradients, in_basis, out_basis):
    seq_here = activations.shape[0] // SEQ_LEN
    size = lax.axis_size("dp")
    seq_total = seq_here * size
    bits = size.bit_length() - 1
    orders = hop_orders(bits)
    swapped = (
        bits > 0
        and size == 1 << bits
        and lax.axis_size("width") == 1
        and in_basis.shape[0] * size % len(orders) == 0
    )
    if not swapped:
        in_rotated, out_rotated = rotate_both(activations, gradients, in_basis, out_basis)
        rotated = outer(in_rotated, out_rotated, seq_here)
        local_mean = (jnp.sum(rotated * rotated, axis=0) / seq_total).astype(jnp.bfloat16)
        eigen_mine = lax.psum_scatter(
            local_mean, "dp", scatter_dimension=0, tiled=True
        ).astype(jnp.float32)
        inverse = lax.all_gather(
            (1.0 / (eigen_mine + damping)).astype(jnp.bfloat16), "dp", axis=0, tiled=True
        )
        return ((rotated * inverse.astype(jnp.float32)).astype(jnp.bfloat16), eigen_mine)
    in_whole = lax.all_gather(in_basis.astype(jnp.bfloat16), "dp", axis=0, tiled=True)
    in_rotated = rotate(activations, in_whole).astype(jnp.bfloat16)
    cols = in_rotated.shape[1]
    eigen_rows, inverse_rows, rotated_rows, sums = [], [], [], None
    for start, stop in row_chunks(out_basis.shape[0]):
        out_part = lax.all_gather(
            out_basis[start:stop].astype(jnp.bfloat16), "dp", axis=0, tiled=True
        )
        tokens = gradients
        if sums is not None:
            tokens, sums = lax.optimization_barrier((gradients, sums))
            eigen_rows[-1] = sums
        out_rotated = rotate(tokens, out_part).astype(jnp.bfloat16)
        rotated = outer(in_rotated, out_rotated, seq_here)
        local_mean = (jnp.sum(rotated * rotated, axis=0) / seq_total).astype(jnp.bfloat16)
        blocks = local_mean.reshape((2,) * bits + (stop - start, cols))
        sums = jnp.concatenate(
            scatter_pieces(
                jnp.split(blocks, len(orders), axis=-1), [(0,) + order[::-1] for order in orders]
            ),
            axis=1,
        )
        inverse_rows.append(
            lax.all_gather(
                (1.0 / (sums + damping)).astype(jnp.bfloat16), "dp", axis=0, tiled=True
            )
        )
        rotated_rows.append(rotated)
        eigen_rows.append(sums)
    scaled_rows = []
    for i, (rotated, inverse) in enumerate(zip(rotated_rows, inverse_rows)):
        if i < len(rotated_rows) - 1:
            rotated, eigen_rows[-1] = lax.optimization_barrier((rotated, eigen_rows[-1]))
        scaled = (rotated * inverse.astype(jnp.float32)).astype(jnp.bfloat16)
        scaled_rows.append(scaled.reshape(seq_here, size, -1, cols))
    preconditioned = jnp.concatenate(scaled_rows, axis=2).reshape(seq_here, -1, cols)
    return (preconditioned, jnp.concatenate(eigen_rows, axis=0))


def solution(mesh):
    placed = (P("dp", "width"), P("dp", "width"), P("dp", "width"), P("dp", "width"))
    return jax.shard_map(
        on_device,
        mesh=mesh,
        in_specs=placed,
        out_specs=(P("dp", None, "width"), P("dp", "width")),
        check_vma=False,
    )
```
